256 devices in a mesh: tm: 32 (over z, x), chan: 8 (over y, core).
Axes of the slice: x: 4, y: 4, z: 8, core: 2. Of those that a mesh axis runs over, the one named last changes fastest.
Arguments:
- voltages: bfloat16 [2, 1024, 128, 512], P(None, 'chan', 'tm'), may hold values from -8 to 8
- chan_order: int32 [8, 128], P('chan'), may hold values from 0 to 127, each once within a row
- flags: int32 [512], replicated, may hold values 0 or 1
- ref_station: int32 [1], replicated, may hold values from 0 to 511
Outputs:
- gains: float32 [1024, 2, 512], P(('tm', 'chan'))
- vis: bfloat16 [1024, 2, 512, 512], P(('tm', 'chan'))
- delays: float32 [2, 512], replicated
The draws below stay inside these ranges and needn't reach their ends.
All inputs are finite; a program needn't handle non-finite values.
Results may differ from the reference program's by a relative error of at most 0.001.
Values may be sent and summed in bfloat16 or wider, within the bound.
No kernel may reach another device: no remote copies, remote signals or barrier semaphores. Data moves between devices by JAX's collectives and lax.ppermute only.
A program may use at most 320 MiB of HBM per device.

```python
import math
import jax
import jax.numpy as jnp
from jax import lax

S = 512
TIME = 128
ITERS = 3
CH_DEV = 4
CHG = 128
CHANS = 1024
N_TM = 32
N_CHAN = 8


def draw_voltages(key, part):
    keys = jax.random.split(key, 7)
    amplitude = jnp.exp(jax.random.uniform(keys[0], (S,), jnp.float32, math.log(0.5), math.log(2.0)))
    rough = jax.random.uniform(keys[1], (CHANS, 1, S), jnp.float32, 0.8, 1.25)
    offset = jax.random.uniform(keys[2], (S,), jnp.float32, -0.6, 0.6)
    slope = jax.random.uniform(keys[3], (S,), jnp.float32, -0.6, 0.6)
    jitter = jax.random.uniform(keys[4], (CHANS, 1, S), jnp.float32, -0.2, 0.2)
    freq = (jnp.arange(CHANS, dtype=jnp.float32) - (CHANS - 1) / 2.0) / CHANS
    phase = offset + 2.0 * slope * freq[:, None, None] + jitter
    gain_real = amplitude * rough * jnp.cos(phase)
    gain_imag = amplitude * rough * jnp.sin(phase)
    source = 0.3 * jax.random.normal(keys[5], (2, CHANS, TIME, 1), jnp.float32)
    noise = jax.random.normal(keys[6], (2, CHANS, TIME, S), jnp.float32)
    volt_real = gain_real * source[0] - gain_imag * source[1] + noise[0]
    volt_imag = gain_real * source[1] + gain_imag * source[0] + noise[1]
    return jnp.clip(jnp.stack([volt_real, volt_imag]), -8.0, 8.0).astype(jnp.bfloat16)


def touch_ends(values, stream_key, low, largest):
    shape = values.shape
    spot = [jax.random.randint(jax.random.fold_in(stream_key, axis), (), 0, shape[axis]) for axis in range(len(shape))]
    values = values.at[tuple(spot)].set(low)
    longest = shape.index(max(shape))
    spot[longest] = (spot[longest] + 1) % shape[longest]
    return values.at[tuple(spot)].set(largest)


def setup_inputs(seed: int = 0) -> dict:
    splits = jax.random.split(jax.random.key(seed), 5)
    return {
        "voltages": draw_voltages(jax.random.fold_in(splits[4], 71), 0),
        "chan_order": jax.vmap(lambda own: jax.random.permutation(own, CHG))(jax.random.split(splits[1], N_CHAN)).reshape((N_CHAN, CHG)).astype(jnp.int32),
        "flags": touch_ends((jax.random.randint(splits[2], (S,), 0, 8) < 7).astype(jnp.int32), jax.random.fold_in(splits[2], 1), 0, 1),
        "ref_station": jax.random.randint(splits[3], (1,), 0, S).astype(jnp.int32),
    }


def visibilities(real_part, imag_part):
    stacked = jnp.concatenate([real_part, imag_part], 0)
    crossed = jnp.concatenate([-imag_part, real_part], 0)
    scale = 1.0 / real_part.shape[0]
    vis_real = jnp.dot(stacked.T, stacked, preferred_element_type=jnp.float32) * scale
    vis_imag = jnp.dot(stacked.T, crossed, preferred_element_type=jnp.float32) * scale
    return vis_real, vis_imag


def stefcal(vis_real, vis_imag, weight):
    high = lax.Precision.HIGHEST
    diag = jnp.diagonal(vis_real)
    gain_real = jnp.ones(weight.shape, jnp.float32)
    gain_imag = jnp.zeros(weight.shape, jnp.float32)
    for sweep in range(ITERS):
        wr = weight * gain_real
        wi = weight * gain_imag
        out_real = jnp.dot(vis_real, wr, precision=high) - jnp.dot(vis_imag, wi, precision=high)
        out_imag = jnp.dot(vis_real, wi, precision=high) + jnp.dot(vis_imag, wr, precision=high)
        numer_real = out_real - diag * wr
        numer_imag = out_imag - diag * wi
        own = weight * (gain_real * gain_real + gain_imag * gain_imag)
        denom = jnp.sum(own) - own + 1e-6
        new_real = numer_real / denom
        new_imag = numer_imag / denom
        if sweep == 1:
            gain_real = 0.5 * (new_real + gain_real)
            gain_imag = 0.5 * (new_imag + gain_imag)
        else:
            gain_real = new_real
            gain_imag = new_imag
    return jnp.stack([gain_real, gain_imag])


def calibrate(real_part, imag_part, weight):
    vis_real, vis_imag = visibilities(real_part, imag_part)
    stored = jnp.stack([vis_real, vis_imag]).astype(jnp.bfloat16)
    return stefcal(vis_real, vis_imag, weight), stored


def fit_stats(gains, freq, ref_station):
    gain_real = gains[:, 0]
    gain_imag = gains[:, 1]
    ref_real = jnp.take(gain_real, ref_station, axis=1)
    ref_imag = jnp.take(gain_imag, ref_station, axis=1)
    power = 0.5 * (gain_real * gain_real + gain_imag * gain_imag + ref_real * ref_real + ref_imag * ref_imag)
    imag_cross = gain_imag * ref_real - gain_real * ref_imag
    fcol = freq[:, None]
    return jnp.stack([jnp.sum(power, 0), jnp.sum(fcol * fcol * power, 0), jnp.sum(imag_cross, 0), jnp.sum(fcol * imag_cross, 0)])


def solve_fit(totals):
    return jnp.stack([totals[2] / totals[0], totals[3] / totals[1]])


def correct(gains, freq, delays):
    angle = delays[0][None, :] + delays[1][None, :] * freq[:, None]
    cosine = jnp.cos(angle)
    sine = jnp.sin(angle)
    gain_real = gains[:, 0]
    gain_imag = gains[:, 1]
    return jnp.stack([gain_real * cosine + gain_imag * sine, gain_imag * cosine - gain_real * sine], 1)


def reference(voltages, chan_order, flags, ref_station):
    weight = flags.astype(jnp.float32)
    group_size = CH_DEV * N_TM

    def one(row):
        tm_index = row // (N_CHAN * CH_DEV)
        group = (row // CH_DEV) % N_CHAN
        within = row % CH_DEV
        local = chan_order[group, tm_index * CH_DEV + within]
        channel = (group * group_size + local).astype(jnp.int32)
        block = lax.dynamic_index_in_dim(voltages, channel, 1, keepdims=False)
        solved, stored = calibrate(block[0], block[1], weight)
        return solved, stored, channel

    gains, vis, channels = lax.map(one, jnp.arange(CHANS, dtype=jnp.int32))
    freq = (channels.astype(jnp.float32) - (CHANS - 1) / 2.0) / CHANS
    delays = solve_fit(fit_stats(gains, freq, ref_station))
    return correct(gains, freq, delays), vis, delays
```

```python
import jax
import jax.numpy as jnp
from jax import lax
from jax.experimental import pallas as pl
from jax.experimental.pallas import tpu as pltpu
from jax.sharding import PartitionSpec as P

ITERS = 3


def pick_kernel(order, volt, out):
    tm, per = out.shape[:2]

    def body(d, _):
        for j in range(per):
            c = order[0, d * per + j]
            out[d, j] = jnp.concatenate([volt[0, c], volt[1, c]], axis=0)
        return 0

    lax.fori_loop(0, tm, body, 0, unroll=2)


def pick(order, volt, tm):
    _, group, tl, stations = volt.shape
    per = group // tm
    return pl.pallas_call(
        pick_kernel,
        out_shape=jax.ShapeDtypeStruct((tm, per, 2 * tl, stations), volt.dtype),
        in_specs=[pl.BlockSpec(memory_space=pltpu.SMEM), pl.BlockSpec(memory_space=pltpu.VMEM)],
        out_specs=pl.BlockSpec(memory_space=pltpu.VMEM),
        name="pick",
    )(order, volt)


def rows_of(real, imag, width):
    row = lax.broadcasted_iota(jnp.int32, (8, width), 0)
    out = jnp.zeros((8, width), jnp.float32)
    for base, value in ((0, real), (3, imag)):
        rest = value
        for k in range(3):
            term = rest.astype(jnp.bfloat16).astype(jnp.float32)
            rest = rest - term
            out = jnp.where(row == base + k, term, out)
    return out.astype(jnp.bfloat16)


def sum_rows(prod):
    row = lax.broadcasted_iota(jnp.int32, prod.shape, 0)
    real = jnp.sum(jnp.where(row < 3, prod, 0.0), 0, keepdims=True)
    imag = jnp.sum(jnp.where(row >= 3, prod, 0.0), 0, keepdims=True)
    return real, imag


def calibrate_kernel(mine, ref, x_ref, flag_ref, vis_ref, gain_ref, stat_ref, s_ref, c_ref, st_ref):
    j = pl.program_id(0)
    src, _, rows, stations = x_ref.shape
    half = src // 2
    time = src * rows // 2
    scale = 1.0 / time
    xf = x_ref[:, 0].astype(jnp.float32)
    low, high = xf[:half], xf[half:]
    sub = lax.broadcasted_iota(jnp.int32, low.shape, 1)
    first = sub < rows // 2
    low_roll = pltpu.roll(low, rows // 2, 1)
    high_roll = pltpu.roll(high, rows // 2, 1)
    real = jnp.where(first, low, high_roll).reshape(time, stations)
    imag = jnp.where(first, low_roll, high).reshape(time, stations)
    diag = (jnp.sum(real * real, 0, keepdims=True) + jnp.sum(imag * imag, 0, keepdims=True)) * scale
    s_ref[:time] = real.astype(jnp.bfloat16)
    s_ref[time:] = imag.astype(jnp.bfloat16)
    c_ref[:time] = (-imag).astype(jnp.bfloat16)
    c_ref[time:] = real.astype(jnp.bfloat16)
    st_ref[:, :time] = real.T.astype(jnp.bfloat16)
    st_ref[:, time:] = imag.T.astype(jnp.bfloat16)

    step = 128
    for r in range(0, stations, step):
        left = st_ref[r : r + step]
        for part, right in ((0, s_ref), (1, c_ref)):
            prod = jnp.dot(left, right[...], preferred_element_type=jnp.float32)
            vis_ref[0, part, r : r + step] = (prod * scale).astype(jnp.bfloat16)

    weight = flag_ref[...].astype(jnp.float32)
    gr = jnp.ones((1, stations), jnp.float32)
    gi = jnp.zeros((1, stations), jnp.float32)
    for sweep in range(ITERS):
        wr = weight * gr
        wi = weight * gi
        prod = jnp.dot(rows_of(wr, wi, stations), st_ref[...], preferred_element_type=jnp.float32)
        sa, sb = sum_rows(prod)
        p = jnp.concatenate([sa[:, :time] + sb[:, time:], sa[:, time:] - sb[:, :time]], 1)
        q = jnp.concatenate([sb[:, :time] - sa[:, time:], sb[:, time:] + sa[:, :time]], 1)
        prod = jnp.dot(rows_of(p, q, 2 * time), s_ref[...], preferred_element_type=jnp.float32)
        yr, yi = sum_rows(prod)
        own = weight * (gr * gr + gi * gi)
        inv = jnp.sum(own, 1, keepdims=True) - own + 1e-6
        hr = (yr * scale - diag * wr) / inv
        hi = (yi * scale - diag * wi) / inv
        if sweep == 1:
            gr, gi = 0.5 * (hr + gr), 0.5 * (hi + gi)
        else:
            gr, gi = hr, hi
    gain_ref[j, 0:1] = gr
    gain_ref[j, 1:2] = gi

    lane = lax.broadcasted_iota(jnp.int32, (1, stations), 1)
    at = lane == ref[0]
    rr = jnp.sum(jnp.where(at, gr, 0.0), 1, keepdims=True)
    ri = jnp.sum(jnp.where(at, gi, 0.0), 1, keepdims=True)
    f = mine[j]
    power = 0.5 * (gr * gr + gi * gi + rr * rr + ri * ri)
    cross = gi * rr - gr * ri
    stats = jnp.concatenate([power, f * f * power, cross, f * cross], 0)

    @pl.when(j == 0)
    def _():
        stat_ref[...] = stats

    @pl.when(j > 0)
    def _():
        stat_ref[...] += stats


def calibrate(freq, ref, turned, flags):
    src, per, rows, stations = turned.shape
    deep = src * rows
    smem = pl.BlockSpec(memory_space=pltpu.SMEM)
    return pl.pallas_call(
        calibrate_kernel,
        grid=(per,),
        out_shape=(
            jax.ShapeDtypeStruct((per, 2, stations, stations), jnp.bfloat16),
            jax.ShapeDtypeStruct((per, 2, stations), jnp.float32),
            jax.ShapeDtypeStruct((4, stations), jnp.float32),
        ),
        in_specs=[
            smem,
            smem,
            pl.BlockSpec((src, 1, rows, stations), lambda j: (0, j, 0, 0)),
            pl.BlockSpec((1, stations), lambda j: (0, 0)),
        ],
        out_specs=(
            pl.BlockSpec((1, 2, stations, stations), lambda j: (j, 0, 0, 0)),
            pl.BlockSpec((per, 2, stations), lambda j: (0, 0, 0)),
            pl.BlockSpec((4, stations), lambda j: (0, 0)),
        ),
        scratch_shapes=[
            pltpu.VMEM((deep, stations), jnp.bfloat16),
            pltpu.VMEM((deep, stations), jnp.bfloat16),
            pltpu.VMEM((stations, deep), jnp.bfloat16),
        ],
        name="calibrate",
    )(freq, ref, turned, flags)


def correct_kernel(freq, total_ref, gain_ref, out_ref, delay_ref):
    offset = total_ref[2:3] / total_ref[0:1]
    slope = total_ref[3:4] / total_ref[1:2]
    delay_ref[0:1] = offset
    delay_ref[1:2] = slope
    for j in range(gain_ref.shape[0]):
        angle = offset + slope * freq[j]
        cosine = jnp.cos(angle)
        sine = jnp.sin(angle)
        gr, gi = gain_ref[j, 0:1], gain_ref[j, 1:2]
        out_ref[j, 0:1] = gr * cosine + gi * sine
        out_ref[j, 1:2] = gi * cosine - gr * sine


def correct(freq, totals, gains):
    smem = pl.BlockSpec(memory_space=pltpu.SMEM)
    vmem = pl.BlockSpec(memory_space=pltpu.VMEM)
    return pl.pallas_call(
        correct_kernel,
        out_shape=(
            jax.ShapeDtypeStruct(gains.shape, jnp.float32),
            jax.ShapeDtypeStruct((2, gains.shape[2]), jnp.float32),
        ),
        in_specs=[smem, vmem, vmem],
        out_specs=(vmem, vmem),
        name="correct",
    )(freq, totals, gains)


def reduce_all(value):
    for axis in ("chan", "tm"):
        n = lax.axis_size(axis)
        copies = lax.optimization_barrier(jnp.broadcast_to(value[None], (n, *value.shape)))
        value = jnp.sum(lax.all_to_all(copies, axis, 0, 0, tiled=True), 0)
    return value


def shards(voltages, chan_order, flags, ref_station):
    tm_count = lax.axis_size("tm")
    group_count = lax.axis_size("chan")
    group_size = voltages.shape[1]
    per = group_size // tm_count
    picked = pick(chan_order, voltages, tm_count)
    turned = lax.all_to_all(picked, "tm", split_axis=0, concat_axis=0, tiled=True)
    mine = lax.dynamic_slice_in_dim(chan_order[0], lax.axis_index("tm") * per, per)
    channels = lax.axis_index("chan") * group_size + mine
    total = group_size * group_count
    freq = (channels.astype(jnp.float32) - (total - 1) / 2.0) / total
    stored, gains, stats = calibrate(freq, ref_station, turned, flags[None])
    totals = reduce_all(stats)
    corrected, delays = correct(freq, totals, gains)
    return (corrected, stored, delays)


def solution(mesh):
    in_specs = (P(None, "chan", "tm", None), P("chan", None), P(), P())
    out_specs = (P(("tm", "chan"), None, None), P(("tm", "chan"), None, None, None), P())
    return jax.shard_map(shards, mesh=mesh, in_specs=in_specs, out_specs=out_specs, check_vma=False)
```

```python
import jax
import jax.numpy as jnp
from jax import lax
from jax.experimental import pallas as pl
from jax.experimental.pallas import tpu as pltpu
from jax.sharding import Mesh
from jax.sharding import PartitionSpec as P

ITERS = 3
CHIPS_X = 4


def pick_kernel(order, volt, out):
    tm, per = out.shape[:2]

    def body(d, _):
        for j in range(per):
            c = order[0, d * per + j]
            out[d, j] = jnp.concatenate([volt[0, c], volt[1, c]], axis=0)
        return 0

    lax.fori_loop(0, tm, body, 0, unroll=2)


def pick(order, volt, tm):
    _, group, tl, stations = volt.shape
    per = group // tm
    return pl.pallas_call(
        pick_kernel,
        out_shape=jax.ShapeDtypeStruct((tm, per, 2 * tl, stations), volt.dtype),
        in_specs=[pl.BlockSpec(memory_space=pltpu.SMEM), pl.BlockSpec(memory_space=pltpu.VMEM)],
        out_specs=pl.BlockSpec(memory_space=pltpu.VMEM),
        compiler_params=pltpu.CompilerParams(vmem_limit_bytes=8 << 20),
        name="pick",
    )(order, volt)


def terms(value):
    out = []
    for _ in range(3):
        term = value.astype(jnp.bfloat16)
        value = value - term.astype(jnp.float32)
        out.append(term.astype(jnp.float32))
    return out


def solve_kernel(freq, ref, x_ref, flag_ref, s_ref, gain_ref, stat_ref):
    src, per, rows, stations = x_ref.shape
    half = src // 2
    time = src * rows // 2
    scale = 1.0 / time
    sub = lax.broadcasted_iota(jnp.int32, (8, stations), 0)
    first = lax.broadcasted_iota(jnp.int32, (half, rows, stations), 1) < rows // 2
    diag = jnp.zeros((8, stations), jnp.float32)
    fcol = jnp.zeros((8, stations), jnp.float32)
    for j in range(per):
        low = x_ref[:half, j].astype(jnp.float32)
        high = x_ref[half:, j].astype(jnp.float32)
        real = jnp.where(first, low, pltpu.roll(high, rows // 2, 1)).reshape(time, stations)
        imag = jnp.where(first, pltpu.roll(low, rows // 2, 1), high).reshape(time, stations)
        s_ref[j, :time] = real.astype(jnp.bfloat16)
        s_ref[j, time:] = imag.astype(jnp.bfloat16)
        power = jnp.sum(real * real + imag * imag, 0, keepdims=True)
        diag = jnp.where(sub == j, power * scale, diag)
        fcol = jnp.where(sub == j, freq[j], fcol)

    def apply(left, contract):
        stacked = jnp.concatenate([t for value in left for t in terms(value)], 0).astype(jnp.bfloat16)
        mixed = None
        for j in range(per):
            prod = lax.dot_general(
                stacked, s_ref[j], (((1,), (contract,)), ((), ())), preferred_element_type=jnp.float32
            )
            row = lax.broadcasted_iota(jnp.int32, prod.shape, 0) % 8
            mixed = jnp.where(row == j, prod, 0.0 if mixed is None else mixed)
        return [mixed[24 * k : 24 * k + 8] + mixed[24 * k + 8 : 24 * k + 16] + mixed[24 * k + 16 : 24 * k + 24] for k in range(2)]

    weight = flag_ref[...].astype(jnp.float32)
    gr = jnp.ones((8, stations), jnp.float32)
    gi = jnp.zeros((8, stations), jnp.float32)
    for sweep in range(ITERS):
        wr = weight * gr
        wi = weight * gi
        sa, sb = apply((wr, wi), 1)
        p = jnp.concatenate([sa[:, :time] + sb[:, time:], sa[:, time:] - sb[:, :time]], 1)
        q = jnp.concatenate([sb[:, :time] - sa[:, time:], sb[:, time:] + sa[:, :time]], 1)
        yr, yi = apply((p, q), 0)
        own = weight * (gr * gr + gi * gi)
        denom = jnp.sum(own, 1, keepdims=True) - own + 1e-6
        hr = (yr * scale - diag * wr) / denom
        hi = (yi * scale - diag * wi) / denom
        if sweep == 1:
            gr, gi = 0.5 * (hr + gr), 0.5 * (hi + gi)
        else:
            gr, gi = hr, hi
    gain_ref[0] = gr
    gain_ref[1] = gi

    at = lax.broadcasted_iota(jnp.int32, (8, stations), 1) == ref[0]
    rr = jnp.sum(jnp.where(at, gr, 0.0), 1, keepdims=True)
    ri = jnp.sum(jnp.where(at, gi, 0.0), 1, keepdims=True)
    power = 0.5 * (gr * gr + gi * gi + rr * rr + ri * ri)
    cross = gi * rr - gr * ri
    live = sub < per
    sums = [
        jnp.sum(jnp.where(live, v, 0.0), 0, keepdims=True)
        for v in (power, fcol * fcol * power, cross, fcol * cross)
    ]
    stats = jnp.concatenate(sums, 0)
    for k in range(stat_ref.shape[0]):
        stat_ref[k] = stats


def solve(freq, ref, turned, flags, copies):
    src, per, rows, stations = turned.shape
    smem = pl.BlockSpec(memory_space=pltpu.SMEM)
    vmem = pl.BlockSpec(memory_space=pltpu.VMEM)
    return pl.pallas_call(
        solve_kernel,
        out_shape=(
            jax.ShapeDtypeStruct((per, src * rows, stations), jnp.bfloat16),
            jax.ShapeDtypeStruct((2, 8, stations), jnp.float32),
            jax.ShapeDtypeStruct((copies, 4, stations), jnp.float32),
        ),
        in_specs=[smem, smem, vmem, vmem],
        out_specs=(vmem, vmem, vmem),
        compiler_params=pltpu.CompilerParams(vmem_limit_bytes=24 << 20),
        name="solve",
    )(freq, ref, turned, flags)


def store_kernel(s_ref, vis_ref):
    deep, stations = s_ref.shape[1:]
    time = deep // 2
    scale = 1.0 / time
    rows = s_ref[0]
    real, imag = rows[:time].astype(jnp.float32), rows[time:].astype(jnp.float32)
    crossed = jnp.concatenate([-imag, real], 0).astype(jnp.bfloat16)
    left = jnp.concatenate([real.T, imag.T], 1).astype(jnp.bfloat16)
    step = 128
    for r in range(0, stations, step):
        for part, right in ((0, rows), (1, crossed)):
            prod = jnp.dot(left[r : r + step], right, preferred_element_type=jnp.float32)
            vis_ref[0, part, r : r + step] = (prod * scale).astype(jnp.bfloat16)


def store(s):
    per, deep, stations = s.shape
    return pl.pallas_call(
        store_kernel,
        grid=(per,),
        out_shape=jax.ShapeDtypeStruct((per, 2, stations, stations), jnp.bfloat16),
        in_specs=[pl.BlockSpec((1, deep, stations), lambda j: (j, 0, 0))],
        out_specs=pl.BlockSpec((1, 2, stations, stations), lambda j: (j, 0, 0, 0)),
        compiler_params=pltpu.CompilerParams(vmem_limit_bytes=24 << 20),
        cost_estimate=pl.CostEstimate(
            flops=per * 4 * stations * stations * deep,
            bytes_accessed=per * stations * (2 * deep + 4 * stations),
            transcendentals=0,
        ),
        name="store",
    )(s)


def correct_kernel(freq, total_ref, gain_ref, out_ref, delay_ref):
    totals = total_ref[0]
    for k in range(1, total_ref.shape[0]):
        totals = totals + total_ref[k]
    offset = totals[2:3] / totals[0:1]
    slope = totals[3:4] / totals[1:2]
    delay_ref[0:1] = offset
    delay_ref[1:2] = slope
    gr, gi = gain_ref[0], gain_ref[1]
    sub = lax.broadcasted_iota(jnp.int32, gr.shape, 0)
    fcol = jnp.zeros(gr.shape, jnp.float32)
    for j in range(out_ref.shape[0]):
        fcol = jnp.where(sub == j, freq[j], fcol)
    angle = offset + slope * fcol
    cosine = jnp.cos(angle)
    sine = jnp.sin(angle)
    real = gr * cosine + gi * sine
    imag = gi * cosine - gr * sine
    for j in range(out_ref.shape[0]):
        out_ref[j, 0:1] = real[j : j + 1]
        out_ref[j, 1:2] = imag[j : j + 1]


def correct(freq, totals, gains, per):
    stations = gains.shape[2]
    smem = pl.BlockSpec(memory_space=pltpu.SMEM)
    vmem = pl.BlockSpec(memory_space=pltpu.VMEM)
    return pl.pallas_call(
        correct_kernel,
        out_shape=(
            jax.ShapeDtypeStruct((per, 2, stations), jnp.float32),
            jax.ShapeDtypeStruct((2, stations), jnp.float32),
        ),
        in_specs=[smem, vmem, vmem],
        out_specs=(vmem, vmem),
        compiler_params=pltpu.CompilerParams(vmem_limit_bytes=8 << 20),
        name="correct",
    )(freq, totals, gains)


def shards(voltages, chan_order, flags, ref_station):
    tm = ("z", "x")
    tm_count = lax.axis_size(tm)
    group_count = lax.axis_size("chan")
    group_size = voltages.shape[1]
    per = group_size // tm_count
    picked = pick(chan_order, voltages, tm_count)
    turned = lax.all_to_all(picked, tm, split_axis=0, concat_axis=0, tiled=True)
    mine = lax.dynamic_slice_in_dim(chan_order[0], lax.axis_index(tm) * per, per)
    channels = lax.axis_index("chan") * group_size + mine
    total = group_size * group_count
    freq = (channels.astype(jnp.float32) - (total - 1) / 2.0) / total
    plane, line = ("x", "chan"), "z"
    s, gains, stats = solve(freq, ref_station, turned, flags[None], lax.axis_size(plane))
    stored = store(s)
    sums = jnp.sum(lax.all_to_all(stats, plane, 0, 0, tiled=True), 0)
    copies = lax.optimization_barrier(jnp.broadcast_to(sums[None], (lax.axis_size(line), *sums.shape)))
    totals = lax.all_to_all(copies, line, 0, 0, tiled=True)
    corrected, delays = correct(freq, totals, gains, per)
    return (corrected, stored, delays)


def solution(mesh):
    tm, chan = mesh.devices.shape
    grid = Mesh(mesh.devices.reshape(tm // CHIPS_X, CHIPS_X, chan), ("z", "x", "chan"))
    tm = ("z", "x")
    in_specs = (P(None, "chan", tm, None), P("chan", None), P(), P())
    out_specs = (P((*tm, "chan"), None, None), P((*tm, "chan"), None, None, None), P())
    return jax.shard_map(shards, mesh=grid, in_specs=in_specs, out_specs=out_specs, check_vma=False)
```

```python
import jax
import jax.numpy as jnp
from jax import lax
from jax.experimental import pallas as pl
from jax.experimental.pallas import tpu as pltpu
from jax.sharding import Mesh
from jax.sharding import PartitionSpec as P

ITERS = 3
CHIPS_X = 4


def pick_kernel(order, volt, out):
    tm, _, pairs = out.shape[:3]

    def body(d, _):
        for pair in range(pairs):
            a = order[0, 2 * (d * pairs + pair)]
            b = order[0, 2 * (d * pairs + pair) + 1]
            for part in range(2):
                out[d, part, pair] = jnp.concatenate([volt[part, a], volt[part, b]], axis=0)
        return 0

    lax.fori_loop(0, tm, body, 0, unroll=2)


def pick(order, volt, tm):
    _, group, tl, stations = volt.shape
    pairs = group // tm // 2
    return pl.pallas_call(
        pick_kernel,
        out_shape=jax.ShapeDtypeStruct((tm, 2, pairs, 2 * tl, stations), volt.dtype),
        in_specs=[pl.BlockSpec(memory_space=pltpu.SMEM), pl.BlockSpec(memory_space=pltpu.VMEM)],
        out_specs=pl.BlockSpec(memory_space=pltpu.VMEM),
        name="pick",
    )(order, volt)


def terms(value):
    out = []
    for _ in range(3):
        term = value.astype(jnp.bfloat16)
        value = value - term.astype(jnp.float32)
        out.append(term.astype(jnp.float32))
    return out


def gather_terms(prod, first):
    return prod[first : first + 8] + prod[first + 8 : first + 16] + prod[first + 16 : first + 24]


def solve_kernel(freq, ref, x_ref, flag_ref, gain_ref, stat_ref):
    src, _, pairs, rows, stations = x_ref.shape
    per = 2 * pairs
    deep = src * rows
    scale = 2.0 / deep
    sub = lax.broadcasted_iota(jnp.int32, (8, stations), 0)
    prow = lax.broadcasted_iota(jnp.int32, (8, deep), 0)
    plane = lax.broadcasted_iota(jnp.int32, (8, deep), 1)
    own_lane = plane // (rows // 2) % 2 == prow % 2
    masks = [jnp.logical_and(prow // 2 == pair, own_lane) for pair in range(pairs)]

    def block(part, pair):
        return x_ref[:, part, pair].reshape(deep, stations)

    def project(left):
        return [
            [
                lax.dot_general(
                    left, block(part, pair), (((1,), (1,)), ((), ())), preferred_element_type=jnp.float32
                )
                for part in range(2)
            ]
            for pair in range(pairs)
        ]

    def back(pq):
        total = None
        for pair in range(pairs):
            for part in range(2):
                left = [t for v in pq[pair][part] for t in terms(jnp.where(masks[pair], v, 0.0))]
                prod = jnp.dot(
                    jnp.concatenate(left, 0).astype(jnp.bfloat16),
                    block(part, pair),
                    preferred_element_type=jnp.float32,
                )
                total = prod if total is None else total + prod
        return gather_terms(total, 0) * scale, gather_terms(total, 24) * scale

    weight = flag_ref[...].astype(jnp.float32)
    gr = jnp.ones((8, stations), jnp.float32)
    gi = jnp.zeros((8, stations), jnp.float32)
    wr = weight * gr
    wi = weight * gi
    diag = None
    for sweep in range(ITERS):
        if sweep == 0:
            pq = [[(r, -i), (i, r)] for r, i in project(wr.astype(jnp.bfloat16))]
        else:
            left = jnp.concatenate(terms(wr) + terms(wi), 0).astype(jnp.bfloat16)
            pq = []
            for real, imag in project(left):
                ar, br = gather_terms(real, 0), gather_terms(real, 24)
                ai, bi = gather_terms(imag, 0), gather_terms(imag, 24)
                pq.append([(ar + bi, br - ai), (ai - br, bi + ar)])
        yr, yi = back(pq)
        if diag is None:
            diag = jnp.zeros((8, stations), jnp.float32)
            for pair in range(pairs):
                power = jnp.zeros((rows, stations), jnp.float32)
                for part in range(2):
                    for t in range(src):
                        tile = x_ref[t, part, pair].astype(jnp.float32)
                        power = power + tile * tile
                half = rows // 2
                for k in range(2):
                    total = jnp.sum(power[k * half : (k + 1) * half], 0, keepdims=True) * scale
                    diag = jnp.where(sub == 2 * pair + k, total, diag)
        own = weight * (gr * gr + gi * gi)
        denom = jnp.sum(own, 1, keepdims=True) - own + 1e-6
        hr = (yr - diag * wr) / denom
        hi = (yi - diag * wi) / denom
        if sweep == 1:
            gr, gi = 0.5 * (hr + gr), 0.5 * (hi + gi)
        else:
            gr, gi = hr, hi
        wr = weight * gr
        wi = weight * gi
    gain_ref[0] = gr
    gain_ref[1] = gi

    fcol = jnp.zeros((8, stations), jnp.float32)
    for j in range(per):
        fcol = jnp.where(sub == j, freq[j], fcol)
    at = lax.broadcasted_iota(jnp.int32, (8, stations), 1) == ref[0]
    rr = jnp.sum(jnp.where(at, gr, 0.0), 1, keepdims=True)
    ri = jnp.sum(jnp.where(at, gi, 0.0), 1, keepdims=True)
    power = 0.5 * (gr * gr + gi * gi + rr * rr + ri * ri)
    cross = gi * rr - gr * ri
    live = sub < per
    sums = [
        jnp.sum(jnp.where(live, v, 0.0), 0, keepdims=True)
        for v in (power, fcol * fcol * power, cross, fcol * cross)
    ]
    stats = jnp.concatenate(sums, 0)
    for k in range(stat_ref.shape[0]):
        stat_ref[k] = stats


def solve(freq, ref, turned, flags, copies):
    stations = turned.shape[-1]
    smem = pl.BlockSpec(memory_space=pltpu.SMEM)
    vmem = pl.BlockSpec(memory_space=pltpu.VMEM)
    return pl.pallas_call(
        solve_kernel,
        out_shape=(
            jax.ShapeDtypeStruct((2, 8, stations), jnp.float32),
            jax.ShapeDtypeStruct((copies, 4, stations), jnp.float32),
        ),
        in_specs=[smem, smem, vmem, vmem],
        out_specs=(vmem, vmem),
        compiler_params=pltpu.CompilerParams(vmem_limit_bytes=24 << 20),
        name="solve",
    )(freq, ref, turned, flags)


def store_kernel(x_ref, vis_ref):
    src, _, _, rows, stations = x_ref.shape
    half = src // 2
    time = src * rows // 2
    scale = 1.0 / time
    first = lax.broadcasted_iota(jnp.int32, (half, rows, stations), 1) < rows // 2
    for k in range(2):
        parts = []
        for part in range(2):
            low = x_ref[:half, part, 0].astype(jnp.float32)
            high = x_ref[half:, part, 0].astype(jnp.float32)
            if k == 0:
                both = jnp.where(first, low, pltpu.roll(high, rows // 2, 1))
            else:
                both = jnp.where(first, pltpu.roll(low, rows // 2, 1), high)
            parts.append(both.reshape(time, stations))
        real, imag = parts
        straight = jnp.concatenate([real, imag], 0).astype(jnp.bfloat16)
        crossed = jnp.concatenate([-imag, real], 0).astype(jnp.bfloat16)
        left = jnp.concatenate([real.T, imag.T], 1).astype(jnp.bfloat16)
        step = 128
        for r in range(0, stations, step):
            for part, right in ((0, straight), (1, crossed)):
                prod = jnp.dot(left[r : r + step], right, preferred_element_type=jnp.float32)
                vis_ref[k, part, r : r + step] = (prod * scale).astype(jnp.bfloat16)


def store(turned):
    src, _, pairs, rows, stations = turned.shape
    per, deep = 2 * pairs, src * rows
    return pl.pallas_call(
        store_kernel,
        grid=(pairs,),
        out_shape=jax.ShapeDtypeStruct((per, 2, stations, stations), jnp.bfloat16),
        in_specs=[pl.BlockSpec((src, 2, 1, rows, stations), lambda i: (0, 0, i, 0, 0))],
        out_specs=pl.BlockSpec((2, 2, stations, stations), lambda i: (i, 0, 0, 0)),
        compiler_params=pltpu.CompilerParams(vmem_limit_bytes=24 << 20),
        cost_estimate=pl.CostEstimate(
            flops=per * 4 * stations * stations * deep,
            bytes_accessed=per * stations * (2 * deep + 4 * stations),
            transcendentals=0,
        ),
        name="store",
    )(turned)


def correct_kernel(freq, total_ref, gain_ref, out_ref, delay_ref):
    totals = total_ref[0]
    for k in range(1, total_ref.shape[0]):
        totals = totals + total_ref[k]
    offset = totals[2:3] / totals[0:1]
    slope = totals[3:4] / totals[1:2]
    delay_ref[0:1] = offset
    delay_ref[1:2] = slope
    gr, gi = gain_ref[0], gain_ref[1]
    sub = lax.broadcasted_iota(jnp.int32, gr.shape, 0)
    fcol = jnp.zeros(gr.shape, jnp.float32)
    for j in range(out_ref.shape[0]):
        fcol = jnp.where(sub == j, freq[j], fcol)
    angle = offset + slope * fcol
    cosine = jnp.cos(angle)
    sine = jnp.sin(angle)
    real = gr * cosine + gi * sine
    imag = gi * cosine - gr * sine
    for j in range(out_ref.shape[0]):
        out_ref[j, 0:1] = real[j : j + 1]
        out_ref[j, 1:2] = imag[j : j + 1]


def correct(freq, totals, gains, per):
    stations = gains.shape[2]
    smem = pl.BlockSpec(memory_space=pltpu.SMEM)
    vmem = pl.BlockSpec(memory_space=pltpu.VMEM)
    return pl.pallas_call(
        correct_kernel,
        out_shape=(
            jax.ShapeDtypeStruct((per, 2, stations), jnp.float32),
            jax.ShapeDtypeStruct((2, stations), jnp.float32),
        ),
        in_specs=[smem, vmem, vmem],
        out_specs=(vmem, vmem),
        compiler_params=pltpu.CompilerParams(vmem_limit_bytes=8 << 20),
        name="correct",
    )(freq, totals, gains)


def shards(voltages, chan_order, flags, ref_station):
    tm = ("z", "x")
    tm_count = lax.axis_size(tm)
    group_count = lax.axis_size("chan")
    group_size = voltages.shape[1]
    per = group_size // tm_count
    picked = pick(chan_order, voltages, tm_count)
    turned = lax.all_to_all(picked, tm, split_axis=0, concat_axis=0, tiled=True)
    mine = lax.dynamic_slice_in_dim(chan_order[0], lax.axis_index(tm) * per, per)
    channels = lax.axis_index("chan") * group_size + mine
    total = group_size * group_count
    freq = (channels.astype(jnp.float32) - (total - 1) / 2.0) / total
    plane, line = ("x", "chan"), "z"
    gains, stats = solve(freq, ref_station, turned, flags[None], lax.axis_size(plane))
    stored = store(turned)
    sums = jnp.sum(lax.all_to_all(stats, plane, 0, 0, tiled=True), 0)
    sums, stored = lax.optimization_barrier((sums, stored))
    copies = lax.optimization_barrier(jnp.broadcast_to(sums[None], (lax.axis_size(line), *sums.shape)))
    totals = lax.all_to_all(copies, line, 0, 0, tiled=True)
    corrected, delays = correct(freq, totals, gains, per)
    return (corrected, stored, delays)


def solution(mesh):
    tm, chan = mesh.devices.shape
    grid = Mesh(mesh.devices.reshape(tm // CHIPS_X, CHIPS_X, chan), ("z", "x", "chan"))
    tm = ("z", "x")
    in_specs = (P(None, "chan", tm, None), P("chan", None), P(), P())
    out_specs = (P((*tm, "chan"), None, None), P((*tm, "chan"), None, None, None), P())
    return jax.shard_map(shards, mesh=grid, in_specs=in_specs, out_specs=out_specs, check_vma=False)
```

```python
import jax
import jax.numpy as jnp
from jax import lax
from jax.experimental import pallas as pl
from jax.experimental.pallas import tpu as pltpu
from jax.sharding import Mesh
from jax.sharding import PartitionSpec as P

ITERS = 3
CHIPS_X = 4


def pick_kernel(order, volt, out):
    tm, _, pairs = out.shape[:3]

    def body(d, _):
        for pair in range(pairs):
            a = order[0, 2 * (d * pairs + pair)]
            b = order[0, 2 * (d * pairs + pair) + 1]
            for part in range(2):
                out[d, part, pair] = jnp.concatenate([volt[part, a], volt[part, b]], axis=0)
        return 0

    lax.fori_loop(0, tm, body, 0, unroll=2)


def pick(order, volt, tm):
    _, group, tl, stations = volt.shape
    pairs = group // tm // 2
    return pl.pallas_call(
        pick_kernel,
        out_shape=jax.ShapeDtypeStruct((tm, 2, pairs, 2 * tl, stations), volt.dtype),
        in_specs=[pl.BlockSpec(memory_space=pltpu.SMEM), pl.BlockSpec(memory_space=pltpu.VMEM)],
        out_specs=pl.BlockSpec(memory_space=pltpu.VMEM),
        name="pick",
    )(order, volt)


def terms(value):
    out = []
    for _ in range(3):
        term = value.astype(jnp.bfloat16)
        value = value - term.astype(jnp.float32)
        out.append(term.astype(jnp.float32))
    return out


def gather_terms(prod, first):
    return prod[first : first + 8] + prod[first + 8 : first + 16] + prod[first + 16 : first + 24]


def solve_kernel(freq, ref, x_ref, flag_ref, gain_ref, stat_ref):
    src, _, pairs, rows, stations = x_ref.shape
    per = 2 * pairs
    deep = src * rows
    scale = 2.0 / deep
    sub = lax.broadcasted_iota(jnp.int32, (8, stations), 0)
    prow = lax.broadcasted_iota(jnp.int32, (8, deep), 0)
    plane = lax.broadcasted_iota(jnp.int32, (8, deep), 1)
    own_lane = plane // (rows // 2) % 2 == prow % 2
    masks = [jnp.logical_and(prow // 2 == pair, own_lane) for pair in range(pairs)]

    def block(part, pair):
        return x_ref[:, part, pair].reshape(deep, stations)

    def project(left):
        return [
            [
                lax.dot_general(
                    left, block(part, pair), (((1,), (1,)), ((), ())), preferred_element_type=jnp.float32
                )
                for part in range(2)
            ]
            for pair in range(pairs)
        ]

    def back(pq):
        total = None
        for pair in range(pairs):
            for part in range(2):
                left = [t for v in pq[pair][part] for t in terms(jnp.where(masks[pair], v, 0.0))]
                prod = jnp.dot(
                    jnp.concatenate(left, 0).astype(jnp.bfloat16),
                    block(part, pair),
                    preferred_element_type=jnp.float32,
                )
                total = prod if total is None else total + prod
        return gather_terms(total, 0) * scale, gather_terms(total, 24) * scale

    weight = flag_ref[...].astype(jnp.float32)
    gr = jnp.ones((8, stations), jnp.float32)
    gi = jnp.zeros((8, stations), jnp.float32)
    wr = weight * gr
    wi = weight * gi
    diag = None
    for sweep in range(ITERS):
        if sweep == 0:
            pq = [[(r, -i), (i, r)] for r, i in project(wr.astype(jnp.bfloat16))]
        else:
            left = jnp.concatenate(terms(wr) + terms(wi), 0).astype(jnp.bfloat16)
            pq = []
            for real, imag in project(left):
                ar, br = gather_terms(real, 0), gather_terms(real, 24)
                ai, bi = gather_terms(imag, 0), gather_terms(imag, 24)
                pq.append([(ar + bi, br - ai), (ai - br, bi + ar)])
        yr, yi = back(pq)
        if diag is None:
            diag = jnp.zeros((8, stations), jnp.float32)
            for pair in range(pairs):
                power = jnp.zeros((rows, stations), jnp.float32)
                for part in range(2):
                    for t in range(src):
                        tile = x_ref[t, part, pair].astype(jnp.float32)
                        power = power + tile * tile
                half = rows // 2
                for k in range(2):
                    total = jnp.sum(power[k * half : (k + 1) * half], 0, keepdims=True) * scale
                    diag = jnp.where(sub == 2 * pair + k, total, diag)
        own = weight * (gr * gr + gi * gi)
        denom = jnp.sum(own, 1, keepdims=True) - own + 1e-6
        hr = (yr - diag * wr) / denom
        hi = (yi - diag * wi) / denom
        if sweep == 1:
            gr, gi = 0.5 * (hr + gr), 0.5 * (hi + gi)
        else:
            gr, gi = hr, hi
        wr = weight * gr
        wi = weight * gi
    gain_ref[0] = gr
    gain_ref[1] = gi

    fcol = jnp.zeros((8, stations), jnp.float32)
    for j in range(per):
        fcol = jnp.where(sub == j, freq[j], fcol)
    at = lax.broadcasted_iota(jnp.int32, (8, stations), 1) == ref[0]
    rr = jnp.sum(jnp.where(at, gr, 0.0), 1, keepdims=True)
    ri = jnp.sum(jnp.where(at, gi, 0.0), 1, keepdims=True)
    power = 0.5 * (gr * gr + gi * gi + rr * rr + ri * ri)
    cross = gi * rr - gr * ri
    live = sub < per
    sums = [
        jnp.sum(jnp.where(live, v, 0.0), 0, keepdims=True)
        for v in (power, fcol * fcol * power, cross, fcol * cross)
    ]
    stats = jnp.concatenate(sums, 0)
    for k in range(stat_ref.shape[0]):
        stat_ref[k] = stats


def solve(freq, ref, turned, flags, copies):
    stations = turned.shape[-1]
    smem = pl.BlockSpec(memory_space=pltpu.SMEM)
    vmem = pl.BlockSpec(memory_space=pltpu.VMEM)
    return pl.pallas_call(
        solve_kernel,
        out_shape=(
            jax.ShapeDtypeStruct((2, 8, stations), jnp.float32),
            jax.ShapeDtypeStruct((copies, 4, stations), jnp.float32),
        ),
        in_specs=[smem, smem, vmem, vmem],
        out_specs=(vmem, vmem),
        compiler_params=pltpu.CompilerParams(vmem_limit_bytes=24 << 20),
        name="solve",
    )(freq, ref, turned, flags)


def store_kernel(x_ref, vis_ref):
    src, _, _, rows, stations = x_ref.shape
    half = src // 2
    time = src * rows // 2
    scale = 1.0 / time
    first = lax.broadcasted_iota(jnp.int32, (half, rows, stations), 1) < rows // 2
    for k in range(2):
        parts = []
        for part in range(2):
            low = x_ref[:half, part, 0].astype(jnp.float32)
            high = x_ref[half:, part, 0].astype(jnp.float32)
            if k == 0:
                both = jnp.where(first, low, pltpu.roll(high, rows // 2, 1))
            else:
                both = jnp.where(first, pltpu.roll(low, rows // 2, 1), high)
            parts.append(both.reshape(time, stations))
        real, imag = parts
        straight = jnp.concatenate([real, imag], 0).astype(jnp.bfloat16)
        crossed = jnp.concatenate([-imag, real], 0).astype(jnp.bfloat16)
        left = jnp.concatenate([real.T, imag.T], 1).astype(jnp.bfloat16)
        step = 128
        for r in range(0, stations, step):
            for part, right in ((0, straight), (1, crossed)):
                prod = jnp.dot(left[r : r + step], right, preferred_element_type=jnp.float32)
                vis_ref[k, part, r : r + step] = (prod * scale).astype(jnp.bfloat16)


def store(turned):
    src, _, pairs, rows, stations = turned.shape
    per, deep = 2 * pairs, src * rows
    return pl.pallas_call(
        store_kernel,
        grid=(pairs,),
        out_shape=jax.ShapeDtypeStruct((per, 2, stations, stations), jnp.bfloat16),
        in_specs=[pl.BlockSpec((src, 2, 1, rows, stations), lambda i: (0, 0, i, 0, 0))],
        out_specs=pl.BlockSpec((2, 2, stations, stations), lambda i: (i, 0, 0, 0)),
        compiler_params=pltpu.CompilerParams(vmem_limit_bytes=24 << 20),
        cost_estimate=pl.CostEstimate(
            flops=per * 4 * stations * stations * deep,
            bytes_accessed=per * stations * (2 * deep + 4 * stations),
            transcendentals=0,
        ),
        name="store",
    )(turned)


def correct_kernel(freq, total_ref, gain_ref, out_ref, delay_ref):
    totals = total_ref[0]
    for k in range(1, total_ref.shape[0]):
        totals = totals + total_ref[k]
    offset = totals[2:3] / totals[0:1]
    slope = totals[3:4] / totals[1:2]
    delay_ref[0:1] = offset
    delay_ref[1:2] = slope
    gr, gi = gain_ref[0], gain_ref[1]
    sub = lax.broadcasted_iota(jnp.int32, gr.shape, 0)
    fcol = jnp.zeros(gr.shape, jnp.float32)
    for j in range(out_ref.shape[0]):
        fcol = jnp.where(sub == j, freq[j], fcol)
    angle = offset + slope * fcol
    cosine = jnp.cos(angle)
    sine = jnp.sin(angle)
    real = gr * cosine + gi * sine
    imag = gi * cosine - gr * sine
    for j in range(out_ref.shape[0]):
        out_ref[j, 0:1] = real[j : j + 1]
        out_ref[j, 1:2] = imag[j : j + 1]


def correct(freq, totals, gains, per):
    stations = gains.shape[2]
    smem = pl.BlockSpec(memory_space=pltpu.SMEM)
    vmem = pl.BlockSpec(memory_space=pltpu.VMEM)
    return pl.pallas_call(
        correct_kernel,
        out_shape=(
            jax.ShapeDtypeStruct((per, 2, stations), jnp.float32),
            jax.ShapeDtypeStruct((2, stations), jnp.float32),
        ),
        in_specs=[smem, vmem, vmem],
        out_specs=(vmem, vmem),
        compiler_params=pltpu.CompilerParams(vmem_limit_bytes=8 << 20),
        name="correct",
    )(freq, totals, gains)


def shards(voltages, chan_order, flags, ref_station):
    tm = ("z", "x")
    tm_count = lax.axis_size(tm)
    group_count = lax.axis_size(("y", "core"))
    group_size = voltages.shape[1]
    per = group_size // tm_count
    picked = pick(chan_order, voltages, tm_count)
    turned = lax.all_to_all(picked, tm, split_axis=0, concat_axis=0, tiled=True)
    mine = lax.dynamic_slice_in_dim(chan_order[0], lax.axis_index(tm) * per, per)
    channels = lax.axis_index(("y", "core")) * group_size + mine
    total = group_size * group_count
    freq = (channels.astype(jnp.float32) - (total - 1) / 2.0) / total
    plane, line = ("x", "y"), "z"
    gains, stats = solve(freq, ref_station, turned, flags[None], 1)
    stats = stats[0]
    stats = stats + lax.ppermute(stats, "core", [(0, 1), (1, 0)])
    stored = store(turned)
    def spread(value, axis):
        copies = jnp.broadcast_to(value[None], (lax.axis_size(axis), *value.shape))
        return lax.all_to_all(lax.optimization_barrier(copies), axis, 0, 0, tiled=True)
    sums = jnp.sum(spread(stats, plane), 0)
    sums, stored = lax.optimization_barrier((sums, stored))
    totals = spread(sums, line)
    corrected, delays = correct(freq, totals, gains, per)
    return (corrected, stored, delays)


def solution(mesh):
    tm, chan = mesh.devices.shape
    grid = Mesh(mesh.devices.reshape(tm // CHIPS_X, CHIPS_X, chan // 2, 2), ("z", "x", "y", "core"))
    chan = ("y", "core")
    tm = ("z", "x")
    in_specs = (P(None, chan, tm, None), P(chan, None), P(), P())
    out_specs = (P((*tm, *chan), None, None), P((*tm, *chan), None, None, None), P())
    return jax.shard_map(shards, mesh=grid, in_specs=in_specs, out_specs=out_specs, check_vma=False)
```

```python
import jax
import jax.numpy as jnp
from jax import lax
from jax.experimental import pallas as pl
from jax.experimental.pallas import tpu as pltpu
from jax.sharding import Mesh
from jax.sharding import PartitionSpec as P

ITERS = 3
CHIPS_X = 4


LANE_STEPS = 1


def pick_kernel(order, volt, out):
    tm, _, pairs = out.shape[:3]

    def body(d, _):
        for pair in range(pairs):
            a = order[0, 2 * (d * pairs + pair)]
            b = order[0, 2 * (d * pairs + pair) + 1]
            out[d, 0, pair] = jnp.concatenate([volt[0, a], volt[0, b]], axis=0)
        return 0

    lax.fori_loop(0, tm, body, 0, unroll=8)


def pick(order, volt, tm):
    parts, group, tl, stations = volt.shape
    pairs = group // tm // 2
    wide = stations // LANE_STEPS
    return pl.pallas_call(
        pick_kernel,
        grid=(parts, LANE_STEPS),
        out_shape=jax.ShapeDtypeStruct((tm, parts, pairs, 2 * tl, stations), volt.dtype),
        in_specs=[
            pl.BlockSpec(memory_space=pltpu.SMEM),
            pl.BlockSpec((1, group, tl, wide), lambda i, k: (i, 0, 0, k)),
        ],
        out_specs=pl.BlockSpec((tm, 1, pairs, 2 * tl, wide), lambda i, k: (0, i, 0, 0, k)),
        name="pick",
    )(order, volt)


def terms(value):
    out = []
    for _ in range(3):
        term = value.astype(jnp.bfloat16)
        value = value - term.astype(jnp.float32)
        out.append(term.astype(jnp.float32))
    return out


def gather_terms(prod, first):
    return prod[first : first + 8] + prod[first + 8 : first + 16] + prod[first + 16 : first + 24]


def solve_kernel(freq, ref, x_ref, flag_ref, gain_ref, stat_ref, s_ref, t_ref):
    src, _, pairs, rows, stations = x_ref.shape
    per = 2 * pairs
    deep = src * rows
    scale = 2.0 / deep
    sub = lax.broadcasted_iota(jnp.int32, (8, stations), 0)
    prow = lax.broadcasted_iota(jnp.int32, (8, deep), 0)
    plane = lax.broadcasted_iota(jnp.int32, (8, deep), 1)
    own_lane = plane // (rows // 2) % 2 == prow % 2
    masks = [jnp.logical_and(prow // 2 == pair, own_lane) for pair in range(pairs)]

    for pair in range(pairs):
        for part in range(2):
            s_ref[pair, part] = x_ref[:, part, pair].reshape(deep, stations)
            t_ref[pair, part] = x_ref[:, part, pair].reshape(deep, stations).T

    def block(part, pair):
        return s_ref[pair, part]

    def project(left):
        return [
            [
                jnp.dot(left, t_ref[pair, part], preferred_element_type=jnp.float32)
                for part in range(2)
            ]
            for pair in range(pairs)
        ]

    def back(pq):
        total = None
        for pair in range(pairs):
            for part in range(2):
                left = [t for v in pq[pair][part] for t in terms(jnp.where(masks[pair], v, 0.0))]
                prod = jnp.dot(
                    jnp.concatenate(left, 0).astype(jnp.bfloat16),
                    block(part, pair),
                    preferred_element_type=jnp.float32,
                )
                total = prod if total is None else total + prod
        return gather_terms(total, 0) * scale, gather_terms(total, 24) * scale

    weight = flag_ref[...].astype(jnp.float32)
    gr = jnp.ones((8, stations), jnp.float32)
    gi = jnp.zeros((8, stations), jnp.float32)
    wr = weight * gr
    wi = weight * gi
    diag = None
    for sweep in range(ITERS):
        if sweep == 0:
            pq = [[(r, -i), (i, r)] for r, i in project(wr.astype(jnp.bfloat16))]
        else:
            left = jnp.concatenate(terms(wr) + terms(wi), 0).astype(jnp.bfloat16)
            pq = []
            for real, imag in project(left):
                ar, br = gather_terms(real, 0), gather_terms(real, 24)
                ai, bi = gather_terms(imag, 0), gather_terms(imag, 24)
                pq.append([(ar + bi, br - ai), (ai - br, bi + ar)])
        yr, yi = back(pq)
        if diag is None:
            diag = jnp.zeros((8, stations), jnp.float32)
            for pair in range(pairs):
                power = jnp.zeros((rows, stations), jnp.float32)
                for part in range(2):
                    for t in range(src):
                        tile = x_ref[t, part, pair].astype(jnp.float32)
                        power = power + tile * tile
                half = rows // 2
                for k in range(2):
                    total = jnp.sum(power[k * half : (k + 1) * half], 0, keepdims=True) * scale
                    diag = jnp.where(sub == 2 * pair + k, total, diag)
        own = weight * (gr * gr + gi * gi)
        denom = jnp.sum(own, 1, keepdims=True) - own + 1e-6
        hr = (yr - diag * wr) / denom
        hi = (yi - diag * wi) / denom
        if sweep == 1:
            gr, gi = 0.5 * (hr + gr), 0.5 * (hi + gi)
        else:
            gr, gi = hr, hi
        wr = weight * gr
        wi = weight * gi
    gain_ref[0] = gr
    gain_ref[1] = gi

    fcol = jnp.zeros((8, stations), jnp.float32)
    for j in range(per):
        fcol = jnp.where(sub == j, freq[j], fcol)
    at = lax.broadcasted_iota(jnp.int32, (8, stations), 1) == ref[0]
    rr = jnp.sum(jnp.where(at, gr, 0.0), 1, keepdims=True)
    ri = jnp.sum(jnp.where(at, gi, 0.0), 1, keepdims=True)
    power = 0.5 * (gr * gr + gi * gi + rr * rr + ri * ri)
    cross = gi * rr - gr * ri
    live = sub < per
    sums = [
        jnp.sum(jnp.where(live, v, 0.0), 0, keepdims=True)
        for v in (power, fcol * fcol * power, cross, fcol * cross)
    ]
    stats = jnp.concatenate(sums, 0)
    for k in range(stat_ref.shape[0]):
        stat_ref[k] = stats


def solve(freq, ref, turned, flags, copies):
    stations = turned.shape[-1]
    smem = pl.BlockSpec(memory_space=pltpu.SMEM)
    vmem = pl.BlockSpec(memory_space=pltpu.VMEM)
    return pl.pallas_call(
        solve_kernel,
        out_shape=(
            jax.ShapeDtypeStruct((2, 8, stations), jnp.float32),
            jax.ShapeDtypeStruct((copies, 4, stations), jnp.float32),
        ),
        in_specs=[smem, smem, vmem, vmem],
        out_specs=(vmem, vmem),
        scratch_shapes=[pltpu.VMEM((turned.shape[2], 2, turned.shape[0] * turned.shape[3], stations), turned.dtype), pltpu.VMEM((turned.shape[2], 2, stations, turned.shape[0] * turned.shape[3]), turned.dtype)],
        compiler_params=pltpu.CompilerParams(vmem_limit_bytes=24 << 20),
        name="solve",
    )(freq, ref, turned, flags)


def store_kernel(x_ref, vis_ref):
    src, _, _, rows, stations = x_ref.shape
    half = src // 2
    time = src * rows // 2
    scale = 1.0 / time
    first = lax.broadcasted_iota(jnp.int32, (half, rows, stations), 1) < rows // 2
    for k in range(2):
        parts = []
        for part in range(2):
            low = x_ref[:half, part, 0].astype(jnp.float32)
            high = x_ref[half:, part, 0].astype(jnp.float32)
            if k == 0:
                both = jnp.where(first, low, pltpu.roll(high, rows // 2, 1))
            else:
                both = jnp.where(first, pltpu.roll(low, rows // 2, 1), high)
            parts.append(both.reshape(time, stations))
        real, imag = parts
        straight = jnp.concatenate([real, imag], 0).astype(jnp.bfloat16)
        crossed = jnp.concatenate([-imag, real], 0).astype(jnp.bfloat16)
        left = jnp.concatenate([real.T, imag.T], 1).astype(jnp.bfloat16)
        step = 128
        for r in range(0, stations, step):
            for part, right in ((0, straight), (1, crossed)):
                prod = jnp.dot(left[r : r + step], right, preferred_element_type=jnp.float32)
                vis_ref[k, part, r : r + step] = (prod * scale).astype(jnp.bfloat16)


def store(turned):
    src, _, pairs, rows, stations = turned.shape
    per, deep = 2 * pairs, src * rows
    return pl.pallas_call(
        store_kernel,
        grid=(pairs,),
        out_shape=jax.ShapeDtypeStruct((per, 2, stations, stations), jnp.bfloat16),
        in_specs=[pl.BlockSpec((src, 2, 1, rows, stations), lambda i: (0, 0, i, 0, 0))],
        out_specs=pl.BlockSpec((2, 2, stations, stations), lambda i: (i, 0, 0, 0)),
        compiler_params=pltpu.CompilerParams(vmem_limit_bytes=24 << 20),
        cost_estimate=pl.CostEstimate(
            flops=per * 4 * stations * stations * deep,
            bytes_accessed=per * stations * (2 * deep + 4 * stations),
            transcendentals=0,
        ),
        name="store",
    )(turned)


def correct_kernel(freq, total_ref, gain_ref, out_ref, delay_ref):
    totals = total_ref[0]
    for k in range(1, total_ref.shape[0]):
        totals = totals + total_ref[k]
    offset = totals[2:3] / totals[0:1]
    slope = totals[3:4] / totals[1:2]
    delay_ref[0:1] = offset
    delay_ref[1:2] = slope
    gr, gi = gain_ref[0], gain_ref[1]
    sub = lax.broadcasted_iota(jnp.int32, gr.shape, 0)
    fcol = jnp.zeros(gr.shape, jnp.float32)
    for j in range(out_ref.shape[0]):
        fcol = jnp.where(sub == j, freq[j], fcol)
    angle = offset + slope * fcol
    cosine = jnp.cos(angle)
    sine = jnp.sin(angle)
    real = gr * cosine + gi * sine
    imag = gi * cosine - gr * sine
    for j in range(out_ref.shape[0]):
        out_ref[j, 0:1] = real[j : j + 1]
        out_ref[j, 1:2] = imag[j : j + 1]


def correct(freq, totals, gains, per):
    stations = gains.shape[2]
    smem = pl.BlockSpec(memory_space=pltpu.SMEM)
    vmem = pl.BlockSpec(memory_space=pltpu.VMEM)
    return pl.pallas_call(
        correct_kernel,
        out_shape=(
            jax.ShapeDtypeStruct((per, 2, stations), jnp.float32),
            jax.ShapeDtypeStruct((2, stations), jnp.float32),
        ),
        in_specs=[smem, vmem, vmem],
        out_specs=(vmem, vmem),
        compiler_params=pltpu.CompilerParams(vmem_limit_bytes=8 << 20),
        name="correct",
    )(freq, totals, gains)


def shards(voltages, chan_order, flags, ref_station):
    tm = ("z", "x")
    tm_count = lax.axis_size(tm)
    group_count = lax.axis_size(("y", "core"))
    group_size = voltages.shape[1]
    per = group_size // tm_count
    picked = pick(chan_order, voltages, tm_count)
    turned = lax.all_to_all(picked, tm, split_axis=0, concat_axis=0, tiled=True)
    mine = lax.dynamic_slice_in_dim(chan_order[0], lax.axis_index(tm) * per, per)
    channels = lax.axis_index(("y", "core")) * group_size + mine
    total = group_size * group_count
    freq = (channels.astype(jnp.float32) - (total - 1) / 2.0) / total
    plane, line = ("x", "y"), "z"
    gains, stats = solve(freq, ref_station, turned, flags[None], 1)
    stats = stats[0]
    stats = stats + lax.ppermute(stats, "core", [(0, 1), (1, 0)])
    stored = store(turned)
    def spread(value, axis):
        copies = jnp.broadcast_to(value[None], (lax.axis_size(axis), *value.shape))
        return lax.all_to_all(lax.optimization_barrier(copies), axis, 0, 0, tiled=True)
    sums = jnp.sum(spread(stats, plane), 0)
    sums, stored = lax.optimization_barrier((sums, stored))
    totals = spread(sums, line)
    corrected, delays = correct(freq, totals, gains, per)
    return (corrected, stored, delays)


def solution(mesh):
    tm, chan = mesh.devices.shape
    grid = Mesh(mesh.devices.reshape(tm // CHIPS_X, CHIPS_X, chan // 2, 2), ("z", "x", "y", "core"))
    chan = ("y", "core")
    tm = ("z", "x")
    in_specs = (P(None, chan, tm, None), P(chan, None), P(), P())
    out_specs = (P((*tm, *chan), None, None), P((*tm, *chan), None, None, None), P())
    return jax.shard_map(shards, mesh=grid, in_specs=in_specs, out_specs=out_specs, check_vma=False)
```

```python
import jax
import jax.numpy as jnp
from jax import lax
from jax.experimental import pallas as pl
from jax.experimental.pallas import tpu as pltpu
from jax.sharding import Mesh
from jax.sharding import PartitionSpec as P

ITERS = 3
CHIPS_X = 4


LANE_STEPS = 1


def pick_kernel(order, volt, out):
    tm, _, pairs = out.shape[:3]

    def body(d, _):
        for pair in range(pairs):
            a = order[0, 2 * (d * pairs + pair)]
            b = order[0, 2 * (d * pairs + pair) + 1]
            out[d, 0, pair] = jnp.concatenate([volt[0, a], volt[0, b]], axis=0)
        return 0

    lax.fori_loop(0, tm, body, 0, unroll=16)


def pick(order, volt, tm):
    parts, group, tl, stations = volt.shape
    pairs = group // tm // 2
    wide = stations // LANE_STEPS
    return pl.pallas_call(
        pick_kernel,
        grid=(parts, LANE_STEPS),
        out_shape=jax.ShapeDtypeStruct((tm, parts, pairs, 2 * tl, stations), volt.dtype),
        in_specs=[
            pl.BlockSpec(memory_space=pltpu.SMEM),
            pl.BlockSpec((1, group, tl, wide), lambda i, k: (i, 0, 0, k)),
        ],
        out_specs=pl.BlockSpec((tm, 1, pairs, 2 * tl, wide), lambda i, k: (0, i, 0, 0, k)),
        name="pick",
    )(order, volt)


def terms(value):
    out = []
    for _ in range(3):
        term = value.astype(jnp.bfloat16)
        value = value - term.astype(jnp.float32)
        out.append(term.astype(jnp.float32))
    return out


def gather_terms(prod, first):
    return prod[first : first + 8] + prod[first + 8 : first + 16] + prod[first + 16 : first + 24]


def solve_kernel(freq, ref, x_ref, flag_ref, gain_ref, stat_ref, s_ref, t_ref):
    src, _, pairs, rows, stations = x_ref.shape
    per = 2 * pairs
    deep = src * rows
    scale = 2.0 / deep
    sub = lax.broadcasted_iota(jnp.int32, (8, stations), 0)
    prow = lax.broadcasted_iota(jnp.int32, (8, deep), 0)
    plane = lax.broadcasted_iota(jnp.int32, (8, deep), 1)
    own_lane = plane // (rows // 2) % 2 == prow % 2
    masks = [jnp.logical_and(prow // 2 == pair, own_lane) for pair in range(pairs)]

    for pair in range(pairs):
        for part in range(2):
            s_ref[pair, part] = x_ref[:, part, pair].reshape(deep, stations)
            t_ref[pair, part] = x_ref[:, part, pair].reshape(deep, stations).T

    def block(part, pair):
        return s_ref[pair, part]

    def project(left):
        return [
            [
                jnp.dot(left, t_ref[pair, part], preferred_element_type=jnp.float32)
                for part in range(2)
            ]
            for pair in range(pairs)
        ]

    def back(pq):
        total = None
        for pair in range(pairs):
            for part in range(2):
                left = [t for v in pq[pair][part] for t in terms(jnp.where(masks[pair], v, 0.0))]
                prod = jnp.dot(
                    jnp.concatenate(left, 0).astype(jnp.bfloat16),
                    block(part, pair),
                    preferred_element_type=jnp.float32,
                )
                total = prod if total is None else total + prod
        return gather_terms(total, 0) * scale, gather_terms(total, 24) * scale

    weight = flag_ref[...].astype(jnp.float32)
    gr = jnp.ones((8, stations), jnp.float32)
    gi = jnp.zeros((8, stations), jnp.float32)
    wr = weight * gr
    wi = weight * gi
    diag = None
    for sweep in range(ITERS):
        if sweep == 0:
            pq = [[(r, -i), (i, r)] for r, i in project(wr.astype(jnp.bfloat16))]
        else:
            left = jnp.concatenate(terms(wr) + terms(wi), 0).astype(jnp.bfloat16)
            pq = []
            for real, imag in project(left):
                ar, br = gather_terms(real, 0), gather_terms(real, 24)
                ai, bi = gather_terms(imag, 0), gather_terms(imag, 24)
                pq.append([(ar + bi, br - ai), (ai - br, bi + ar)])
        yr, yi = back(pq)
        if diag is None:
            diag = jnp.zeros((8, stations), jnp.float32)
            for pair in range(pairs):
                power = jnp.zeros((rows, stations), jnp.float32)
                for part in range(2):
                    for t in range(src):
                        tile = x_ref[t, part, pair].astype(jnp.float32)
                        power = power + tile * tile
                half = rows // 2
                for k in range(2):
                    total = jnp.sum(power[k * half : (k + 1) * half], 0, keepdims=True) * scale
                    diag = jnp.where(sub == 2 * pair + k, total, diag)
        own = weight * (gr * gr + gi * gi)
        denom = jnp.sum(own, 1, keepdims=True) - own + 1e-6
        hr = (yr - diag * wr) / denom
        hi = (yi - diag * wi) / denom
        if sweep == 1:
            gr, gi = 0.5 * (hr + gr), 0.5 * (hi + gi)
        else:
            gr, gi = hr, hi
        wr = weight * gr
        wi = weight * gi
    gain_ref[0] = gr
    gain_ref[1] = gi

    fcol = jnp.zeros((8, stations), jnp.float32)
    for j in range(per):
        fcol = jnp.where(sub == j, freq[j], fcol)
    at = lax.broadcasted_iota(jnp.int32, (8, stations), 1) == ref[0]
    rr = jnp.sum(jnp.where(at, gr, 0.0), 1, keepdims=True)
    ri = jnp.sum(jnp.where(at, gi, 0.0), 1, keepdims=True)
    power = 0.5 * (gr * gr + gi * gi + rr * rr + ri * ri)
    cross = gi * rr - gr * ri
    live = sub < per
    sums = [
        jnp.sum(jnp.where(live, v, 0.0), 0, keepdims=True)
        for v in (power, fcol * fcol * power, cross, fcol * cross)
    ]
    stats = jnp.concatenate(sums, 0)
    for k in range(stat_ref.shape[0]):
        stat_ref[k] = stats


def solve(freq, ref, turned, flags, copies):
    stations = turned.shape[-1]
    smem = pl.BlockSpec(memory_space=pltpu.SMEM)
    vmem = pl.BlockSpec(memory_space=pltpu.VMEM)
    return pl.pallas_call(
        solve_kernel,
        out_shape=(
            jax.ShapeDtypeStruct((2, 8, stations), jnp.float32),
            jax.ShapeDtypeStruct((copies, 4, stations), jnp.float32),
        ),
        in_specs=[smem, smem, vmem, vmem],
        out_specs=(vmem, vmem),
        scratch_shapes=[pltpu.VMEM((turned.shape[2], 2, turned.shape[0] * turned.shape[3], stations), turned.dtype), pltpu.VMEM((turned.shape[2], 2, stations, turned.shape[0] * turned.shape[3]), turned.dtype)],
        compiler_params=pltpu.CompilerParams(vmem_limit_bytes=24 << 20),
        name="solve",
    )(freq, ref, turned, flags)


def store_kernel(x_ref, vis_ref):
    src, _, _, rows, stations = x_ref.shape
    half = src // 2
    time = src * rows // 2
    scale = 1.0 / time
    first = lax.broadcasted_iota(jnp.int32, (half, rows, stations), 1) < rows // 2
    for k in range(2):
        parts = []
        for part in range(2):
            low = x_ref[:half, part, 0].astype(jnp.float32)
            high = x_ref[half:, part, 0].astype(jnp.float32)
            if k == 0:
                both = jnp.where(first, low, pltpu.roll(high, rows // 2, 1))
            else:
                both = jnp.where(first, pltpu.roll(low, rows // 2, 1), high)
            parts.append(both.reshape(time, stations))
        real, imag = parts
        straight = jnp.concatenate([real, imag], 0).astype(jnp.bfloat16)
        crossed = jnp.concatenate([-imag, real], 0).astype(jnp.bfloat16)
        left = jnp.concatenate([real.T, imag.T], 1).astype(jnp.bfloat16)
        step = 128
        for r in range(0, stations, step):
            for part, right in ((0, straight), (1, crossed)):
                prod = jnp.dot(left[r : r + step], right, preferred_element_type=jnp.float32)
                vis_ref[k, part, r : r + step] = (prod * scale).astype(jnp.bfloat16)


def store(turned):
    src, _, pairs, rows, stations = turned.shape
    per, deep = 2 * pairs, src * rows
    return pl.pallas_call(
        store_kernel,
        grid=(pairs,),
        out_shape=jax.ShapeDtypeStruct((per, 2, stations, stations), jnp.bfloat16),
        in_specs=[pl.BlockSpec((src, 2, 1, rows, stations), lambda i: (0, 0, i, 0, 0))],
        out_specs=pl.BlockSpec((2, 2, stations, stations), lambda i: (i, 0, 0, 0)),
        compiler_params=pltpu.CompilerParams(vmem_limit_bytes=24 << 20),
        cost_estimate=pl.CostEstimate(
            flops=per * 4 * stations * stations * deep,
            bytes_accessed=per * stations * (2 * deep + 4 * stations),
            transcendentals=0,
        ),
        name="store",
    )(turned)


def correct_kernel(freq, total_ref, gain_ref, out_ref, delay_ref):
    totals = total_ref[0]
    for k in range(1, total_ref.shape[0]):
        totals = totals + total_ref[k]
    offset = totals[2:3] / totals[0:1]
    slope = totals[3:4] / totals[1:2]
    delay_ref[0:1] = offset
    delay_ref[1:2] = slope
    gr, gi = gain_ref[0], gain_ref[1]
    sub = lax.broadcasted_iota(jnp.int32, gr.shape, 0)
    fcol = jnp.zeros(gr.shape, jnp.float32)
    for j in range(out_ref.shape[0]):
        fcol = jnp.where(sub == j, freq[j], fcol)
    angle = offset + slope * fcol
    cosine = jnp.cos(angle)
    sine = jnp.sin(angle)
    real = gr * cosine + gi * sine
    imag = gi * cosine - gr * sine
    for j in range(out_ref.shape[0]):
        out_ref[j, 0:1] = real[j : j + 1]
        out_ref[j, 1:2] = imag[j : j + 1]


def correct(freq, totals, gains, per):
    stations = gains.shape[2]
    smem = pl.BlockSpec(memory_space=pltpu.SMEM)
    vmem = pl.BlockSpec(memory_space=pltpu.VMEM)
    return pl.pallas_call(
        correct_kernel,
        out_shape=(
            jax.ShapeDtypeStruct((per, 2, stations), jnp.float32),
            jax.ShapeDtypeStruct((2, stations), jnp.float32),
        ),
        in_specs=[smem, vmem, vmem],
        out_specs=(vmem, vmem),
        compiler_params=pltpu.CompilerParams(vmem_limit_bytes=8 << 20),
        name="correct",
    )(freq, totals, gains)


def shards(voltages, chan_order, flags, ref_station):
    tm = ("z", "x")
    tm_count = lax.axis_size(tm)
    group_count = lax.axis_size(("y", "core"))
    group_size = voltages.shape[1]
    per = group_size // tm_count
    picked = pick(chan_order, voltages, tm_count)
    turned = lax.all_to_all(picked, tm, split_axis=0, concat_axis=0, tiled=True)
    mine = lax.dynamic_slice_in_dim(chan_order[0], lax.axis_index(tm) * per, per)
    channels = lax.axis_index(("y", "core")) * group_size + mine
    total = group_size * group_count
    freq = (channels.astype(jnp.float32) - (total - 1) / 2.0) / total
    plane, line = ("x", "y"), "z"
    gains, stats = solve(freq, ref_station, turned, flags[None], 1)
    stats = stats[0]
    stats = stats + lax.ppermute(stats, "core", [(0, 1), (1, 0)])
    stored = store(turned)
    def spread(value, axis):
        copies = jnp.broadcast_to(value[None], (lax.axis_size(axis), *value.shape))
        return lax.all_to_all(lax.optimization_barrier(copies), axis, 0, 0, tiled=True)
    sums = jnp.sum(spread(stats, plane), 0)
    sums, stored = lax.optimization_barrier((sums, stored))
    totals = spread(sums, line)
    corrected, delays = correct(freq, totals, gains, per)
    return (corrected, stored, delays)


def solution(mesh):
    tm, chan = mesh.devices.shape
    grid = Mesh(mesh.devices.reshape(tm // CHIPS_X, CHIPS_X, chan // 2, 2), ("z", "x", "y", "core"))
    chan = ("y", "core")
    tm = ("z", "x")
    in_specs = (P(None, chan, tm, None), P(chan, None), P(), P())
    out_specs = (P((*tm, *chan), None, None), P((*tm, *chan), None, None, None), P())
    return jax.shard_map(shards, mesh=grid, in_specs=in_specs, out_specs=out_specs, check_vma=False)
```
